32 devices in a mesh: blk: 8 (over y, x, core), rows: 4 (over z).
Axes of the slice: x: 2, y: 2, z: 4, core: 2. Of those that a mesh axis runs over, the one named last changes fastest.
Arguments:
- cholesky: bfloat16 [4096, 256, 256], P('blk', 'rows'), may hold values from -0.01171875 to 0.01171875
- green: bfloat16 [256, 256, 256], P('blk', 'rows'), may hold values from -18 to 18
- aux_field: float32 [256, 4096], P(None, 'blk'), may hold values from -6 to 6
- walker_orbitals: bfloat16 [256, 256, 128], P('blk', 'rows'), may hold values from -6 to 6
Outputs:
- new_orbitals: float32 [256, 256, 128], P('blk', 'rows')
- force_bias: float32 [256, 4096], P(None, 'blk')
The draws below stay inside these ranges and needn't reach their ends.
All inputs are finite; a program needn't handle non-finite values.
Results may differ from the reference program's by a relative error of at most 0.025.
Values may be sent and summed in bfloat16 or wider, within the bound.
No kernel may reach another device: no remote copies, remote signals or barrier semaphores. Data moves between devices by JAX's collectives and lax.ppermute only.
A program may use at most 128 MiB of HBM per device.

```python
import jax
import jax.numpy as jnp
from jax import lax

N = 256
NOCC = 128
CH_DEV = 512
TAYLOR = 4
CHOL = 4096
WALKERS = 256
N_BLK = 8


def shard_levels(own_key, shape, cuts, least, largest):
    factor_of = 1.0
    for position, parts in cuts:
        steps = jax.random.uniform(jax.random.fold_in(jax.random.fold_in(own_key, 6), position), (parts,), jnp.float32, least / len(cuts), largest / len(cuts))
        factor_of = factor_of * jnp.repeat(jnp.exp(steps), shape[position] // parts).reshape((-1,) + (1,) * (len(shape) - 1 - position))
    return factor_of


def centred(key, dims, deviation, limit, cuts=(), kind=jnp.bfloat16):
    entries = deviation * jax.random.normal(key, dims, jnp.float32)
    if cuts:
        entries = entries * shard_levels(key, dims, cuts, -0.22, 0.18)
    return jnp.clip(entries, -limit, limit).astype(kind)


def setup_inputs(seed: int = 0) -> dict:
    keys = jax.random.split(jax.random.key(seed), 5)
    cholesky = centred(keys[0], (CHOL, N, N), (N * CHOL // 4) ** -0.5, 0.01171875, ((0, 8), (1, 4)))
    green = centred(keys[1], (WALKERS, N, N), 3.0, 18.0, ((0, 8), (1, 4)))
    aux_field = centred(keys[2], (WALKERS, CHOL), 1.0, 6.0, ((1, 8),), jnp.float32)
    walker_orbitals = centred(keys[3], (WALKERS, N, NOCC), 1.0, 6.0, ((0, 8), (1, 4)))
    return dict(cholesky=cholesky, green=green, aux_field=aux_field, walker_orbitals=walker_orbitals)


time_root = 0.5


def reference(cholesky, green, aux_field, walker_orbitals):
    flat_chol = cholesky.reshape(CHOL, N * N)
    flat_green = green.reshape(WALKERS, N * N)
    force_bias = lax.dot_general(flat_green, flat_chol, (((1,), (1,)), ((), ())), preferred_element_type=jnp.float32)
    shifted = (time_root * (aux_field - force_bias)).astype(jnp.bfloat16)

    def add_block(block, summed):
        first_vec = (block * CH_DEV).astype(jnp.int32)
        field_cols = lax.dynamic_slice_in_dim(shifted, first_vec, CH_DEV, 1)
        chol_rows = lax.dynamic_slice_in_dim(flat_chol, first_vec, CH_DEV, 0)
        partial_value = jnp.dot(field_cols, chol_rows, preferred_element_type=jnp.float32)
        return summed + partial_value.astype(jnp.bfloat16).astype(jnp.float32)

    summed = lax.fori_loop(0, N_BLK, add_block, jnp.zeros((WALKERS, N * N), jnp.float32))
    potential = summed.astype(jnp.bfloat16).reshape(WALKERS, N, N)
    taylor_term = walker_orbitals
    result = walker_orbitals.astype(jnp.float32)
    for degree in range(1, TAYLOR + 1):
        product = jnp.einsum("wik,wka->wia", potential.astype(jnp.float32), taylor_term.astype(jnp.float32))
        taylor_term = (product / degree).astype(jnp.bfloat16)
        result = result + taylor_term.astype(jnp.float32)
    return result, force_bias
```

```python
import functools

import jax
import jax.numpy as jnp
from jax import lax
from jax.experimental import pallas as pl
from jax.experimental.pallas import tpu as pltpu
from jax.sharding import PartitionSpec as P

TAYLOR = 4
CHUNKS = 1

time_root = 0.5
F32, BF16 = jnp.float32, jnp.bfloat16


def spread(core, rel, bits):
    if core == 0:
        return rel
    return sum(((rel >> t) & 1) << (bits - 1 - t) for t in range(bits))


def vmem_limit():
    return pltpu.CompilerParams(vmem_limit_bytes=56 << 20)


def bias_kernel(order, *refs, pieces, steps):
    greens, (kept, swapped, out_kept, out_sent, acc_kept, acc_sent) = refs[:pieces], refs[pieces:]
    step = pl.program_id(0)
    depth = kept.shape[0]
    lhs = jnp.concatenate(
        [jnp.concatenate([g[i] for g in greens], axis=0) for i in range(depth)], axis=1
    )
    for chol, acc in ((kept, acc_kept), (swapped, acc_sent)):
        rhs = jnp.concatenate([chol[i] for i in range(depth)], axis=1)
        part = lax.dot_general(lhs, rhs, (((1,), (1,)), ((), ())), preferred_element_type=F32)

        @pl.when(step == 0)
        def _():
            acc[...] = part

        @pl.when(step > 0)
        def _():
            acc[...] += part

    @pl.when(step == steps - 1)
    def _():
        blocks = 2 * pieces
        rows = acc_kept.shape[0] // blocks
        for b in range(blocks):
            to = pl.ds(pl.multiple_of(order[b] * rows, rows), rows)
            out_kept[to, :] = acc_kept[b * rows : (b + 1) * rows, :].astype(out_kept.dtype)
            out_sent[to, :] = acc_sent[b * rows : (b + 1) * rows, :].astype(out_sent.dtype)


def bias_parts(order, greens, kept, swapped):
    rows, vecs, orbitals = kept.shape
    pieces = len(greens)
    walkers = pieces * greens[0].shape[1]
    depth = 4
    steps = rows // depth
    chol_spec = pl.BlockSpec((depth, vecs, orbitals), lambda i, o: (i, 0, 0))
    green_spec = pl.BlockSpec((depth,) + greens[0].shape[1:], lambda i, o: (i, 0, 0))
    out_spec = pl.BlockSpec((walkers, vecs), lambda i, o: (0, 0))
    return pl.pallas_call(
        functools.partial(bias_kernel, pieces=pieces, steps=steps),
        out_shape=(
            jax.ShapeDtypeStruct((walkers, vecs), F32),
            jax.ShapeDtypeStruct((walkers, vecs), BF16),
        ),
        grid_spec=pltpu.PrefetchScalarGridSpec(
            num_scalar_prefetch=1,
            grid=(steps,),
            in_specs=[green_spec] * pieces + [chol_spec] * 2,
            out_specs=(out_spec, out_spec),
            scratch_shapes=[pltpu.VMEM((walkers, vecs), F32)] * 2,
        ),
        cost_estimate=pl.CostEstimate(
            flops=4 * walkers * rows * vecs * orbitals,
            bytes_accessed=4 * rows * vecs * orbitals + 2 * walkers * rows * orbitals,
            transcendentals=0,
        ),
        compiler_params=vmem_limit(),
        name="bias",
    )(order, *greens, kept, swapped)


def potential_kernel(order, *refs, pieces):
    shift_kept, shift_swapped, kept, swapped = refs[:4]
    outs, (field,) = refs[4 : 4 + pieces], refs[4 + pieces :]
    vecs = shift_kept.shape[1]
    blocks = 2 * pieces
    rows = field.shape[0] // blocks

    @pl.when(pl.program_id(0) == 0)
    def _():
        for b in range(blocks):
            at = pl.ds(pl.multiple_of(order[b] * rows, rows), rows)
            field[b * rows : (b + 1) * rows, :vecs] = shift_kept[at, :]
            field[b * rows : (b + 1) * rows, vecs:] = shift_swapped[at, :]

    for i in range(kept.shape[0]):
        rhs = jnp.concatenate([kept[i], swapped[i]], axis=0)
        part = jnp.dot(field[...], rhs, preferred_element_type=F32).astype(BF16)
        for j, out in enumerate(outs):
            out[i] = part[2 * j * rows : 2 * (j + 1) * rows]


def potential_parts(order, shift_kept, shift_swapped, kept, swapped, pieces):
    rows, vecs, orbitals = kept.shape
    walkers = shift_kept.shape[0]
    depth = 4
    chol_spec = pl.BlockSpec((depth, vecs, orbitals), lambda i, o: (i, 0, 0))
    shift_spec = pl.BlockSpec((walkers, vecs), lambda i, o: (0, 0))
    per = walkers // pieces
    return pl.pallas_call(
        functools.partial(potential_kernel, pieces=pieces),
        out_shape=[jax.ShapeDtypeStruct((rows, per, orbitals), BF16)] * pieces,
        grid_spec=pltpu.PrefetchScalarGridSpec(
            num_scalar_prefetch=1,
            grid=(rows // depth,),
            in_specs=[shift_spec] * 2 + [chol_spec] * 2,
            out_specs=[pl.BlockSpec((depth, per, orbitals), lambda i, o: (i, 0, 0))] * pieces,
            scratch_shapes=[pltpu.VMEM((walkers, 2 * vecs), BF16)],
        ),
        cost_estimate=pl.CostEstimate(
            flops=4 * walkers * rows * vecs * orbitals,
            bytes_accessed=4 * rows * vecs * orbitals + 2 * walkers * rows * orbitals,
            transcendentals=0,
        ),
        compiler_params=vmem_limit(),
        name="potential",
    )(order, shift_kept, shift_swapped, kept, swapped)


def taylor_kernel(order, *refs, groups):
    pots, terms = refs[: 2 * groups], refs[2 * groups : 3 * groups]
    outs = refs[3 * groups : 4 * groups]
    full_pot, full_term, full_sum = refs[4 * groups :]
    low = pots[0].shape[1]
    high = terms[0].shape[1]
    for b, piece in enumerate(pots):
        full_pot[:, pl.ds(pl.multiple_of(order[b] * low, low), low), :] = piece[...]
    for s, piece in enumerate(terms):
        at = pl.ds(pl.multiple_of((order[2 * s] // 2) * high, high), high)
        full_term[:, at, :] = piece[...]
    for w in range(full_pot.shape[0]):
        pot = full_pot[w]
        term = full_term[w]
        total = None
        for degree in range(1, TAYLOR + 1):
            product = jnp.dot(pot, term, preferred_element_type=F32)
            term = (product / degree).astype(BF16)
            total = term.astype(F32) if total is None else total + term.astype(F32)
        full_sum[w] = total.astype(BF16)
    for s, out in enumerate(outs):
        at = pl.ds(pl.multiple_of((order[2 * s] // 2) * high, high), high)
        out[...] = full_sum[:, at, :]


def taylor_sums(order, pots, terms):
    groups = len(terms)
    count, low, orbitals = pots[0].shape
    high, occupied = terms[0].shape[1:]
    vmem = pl.BlockSpec(memory_space=pltpu.VMEM)
    return pl.pallas_call(
        functools.partial(taylor_kernel, groups=groups),
        out_shape=[jax.ShapeDtypeStruct((count, high, occupied), BF16)] * groups,
        in_specs=[pl.BlockSpec(memory_space=pltpu.SMEM)] + [vmem] * (3 * groups),
        out_specs=[vmem] * groups,
        scratch_shapes=[
            pltpu.VMEM((count, orbitals, orbitals), BF16),
            pltpu.VMEM((count, orbitals, occupied), BF16),
            pltpu.VMEM((count, orbitals, occupied), BF16),
        ],
        cost_estimate=pl.CostEstimate(
            flops=2 * TAYLOR * count * orbitals * orbitals * occupied,
            bytes_accessed=2 * count * orbitals * (orbitals + 2 * occupied),
            transcendentals=0,
        ),
        compiler_params=vmem_limit(),
        name="taylor",
    )(order, *pots, *terms)


def shards(cholesky, green, aux_field, walker_orbitals):
    n_blk, n_rows = lax.axis_size("blk"), lax.axis_size("rows")
    me, plane = lax.axis_index("blk"), lax.axis_index("rows")
    core = me & 1
    vecs, rows_dev, orbitals = cholesky.shape
    walk_count, _, occupied = walker_orbitals.shape
    half = rows_dev // 2
    chips = n_blk // 2
    bits = chips.bit_length() - 1
    mine = walk_count // CHUNKS
    each = mine // n_rows

    def swap_cores(x):
        return lax.ppermute(x, "blk", [(i, i ^ 1) for i in range(n_blk)])

    def swap_chips(x, t):
        pairs = [(i, i ^ (spread(i & 1, 1 << t, bits) << 1)) for i in range(n_blk)]
        return lax.ppermute(x, "blk", pairs)

    def swap_planes(x, s, h=0):
        pairs = [
            (b * n_rows + z, (b ^ h) * n_rows + (z ^ s)) for b in range(n_blk) for z in range(n_rows)
        ]
        return lax.ppermute(x, ("blk", "rows"), pairs)

    tables = [
        [(spread(c, j, bits) << 1) | h for j in range(chips) for h in range(2)] for c in range(2)
    ]
    order = me ^ jnp.where(core == 0, jnp.array(tables[0], jnp.int32), jnp.array(tables[1], jnp.int32))
    plane_order = (plane * 2 + core) ^ jnp.arange(2 * n_rows, dtype=jnp.int32)

    def row_half(x, which):
        part = lax.dynamic_slice_in_dim(x, which * half, half, 1)
        return part.transpose(1, 0, 2)

    green_kept = row_half(green, core)
    green_sent = row_half(green, 1 - core)
    green_swapped = swap_cores(green_sent)
    chol_sent = row_half(cholesky, 1 - core)
    chol_swapped = swap_cores(chol_sent)
    chol_kept = row_half(cholesky, core)

    results, biases = [], []
    for chunk in range(CHUNKS):
        first = chunk * mine
        gathered = [
            jnp.concatenate(
                [green_kept[:, first : first + mine], green_swapped[:, first : first + mine]], axis=1
            )
        ]
        for t in range(bits):
            gathered += [swap_chips(piece, t) for piece in gathered]

        own = walker_orbitals[first : first + mine].reshape(n_rows, each, rows_dev, occupied)
        terms = [
            swap_planes(lax.dynamic_index_in_dim(own, plane ^ s, 0, keepdims=False), s) if s
            else lax.dynamic_index_in_dim(own, plane, 0, keepdims=False)
            for s in range(n_rows)
        ]

        bias_kept, bias_sent = bias_parts(order, gathered, chol_kept, chol_swapped)
        walkers = bias_kept.shape[0]
        bias_chip = (bias_kept + swap_cores(bias_sent).astype(F32)).astype(BF16)
        parts = bias_chip.reshape(n_rows, walkers // n_rows, vecs)
        quarter = sum(
            (swap_planes(lax.dynamic_index_in_dim(parts, plane ^ s, 0, keepdims=False), s)
             if s else lax.dynamic_index_in_dim(parts, plane, 0, keepdims=False)).astype(F32)
            for s in range(n_rows)
        ).astype(BF16)
        bias = jnp.zeros((n_rows, walkers // n_rows, vecs), BF16)
        for s in range(n_rows):
            got = swap_planes(quarter, s) if s else quarter
            bias = lax.dynamic_update_index_in_dim(bias, got, plane ^ s, 0)
        bias = bias.reshape(walkers, vecs).astype(F32)
        biases.append(bias)
        aux = aux_field.reshape(n_blk, walk_count, vecs)[:, first : first + mine].reshape(walkers, vecs)
        shifted = (time_root * (aux - bias)).astype(BF16)
        shifted_swapped = swap_cores(shifted)

        acc = list(potential_parts(order, shifted, shifted_swapped, chol_kept, chol_swapped, chips))
        total = [a.astype(F32) for a in acc]
        for t in reversed(range(bits)):
            for j in reversed(range(1 << t)):
                sent = total[j + (1 << t)].astype(BF16)
                total[j] = total[j] + swap_chips(sent, t).astype(F32)
        potential = total[0].astype(BF16).transpose(1, 0, 2)
        potential = potential.reshape(2, n_rows, each, half, orbitals)
        pots = []
        for s in range(n_rows):
            for h in range(2):
                piece = lax.dynamic_index_in_dim(potential[h], plane ^ s, 0, keepdims=False)
                if s:
                    piece = swap_planes(piece, s, h)
                elif h:
                    piece = swap_cores(piece)
                pots.append(piece)
        sums = taylor_sums(plane_order, pots, terms)
        result = jnp.zeros((n_rows, each, rows_dev, occupied), BF16)
        for s in range(n_rows):
            got = swap_planes(sums[s], s) if s else sums[s]
            result = lax.dynamic_update_index_in_dim(result, got, plane ^ s, 0)
        result = result.reshape(mine, rows_dev, occupied)
        results.append(walker_orbitals[first : first + mine].astype(F32) + result.astype(F32))

    new_orbitals = jnp.concatenate(results, axis=0)
    force_bias = jnp.stack([b.reshape(n_blk, mine, vecs) for b in biases], axis=1)
    return new_orbitals, force_bias.reshape(n_blk * walk_count, vecs)


def solution(mesh):
    return jax.shard_map(
        shards,
        mesh=mesh,
        in_specs=(
            P("blk", "rows", None),
            P("blk", "rows", None),
            P(None, "blk"),
            P("blk", "rows", None),
        ),
        out_specs=(P("blk", "rows", None), P(None, "blk")),
        check_vma=False,
    )
```

```python
import functools

import jax
import jax.numpy as jnp
from jax import lax
from jax.experimental import pallas as pl
from jax.experimental.pallas import tpu as pltpu
from jax.sharding import PartitionSpec as P


TAYLOR = 4
CHUNKS = 2
PARTS = 2

time_root = 0.5
F32, BF16 = jnp.float32, jnp.bfloat16


def spread(core, rel, bits):
    if core == 0:
        return rel
    return sum(((rel >> t) & 1) << (bits - 1 - t) for t in range(bits))


def vmem_limit():
    return pltpu.CompilerParams(vmem_limit_bytes=56 << 20)


def relayout_kernel(which, block, out):
    out[...] = jnp.swapaxes(block[...], 0, 1)


def vectors_inner(cholesky, which, part):
    vecs, rows, orbitals = cholesky.shape
    half = rows // 2 // PARTS
    depth, width = min(16, half), min(256, vecs)
    which = (which * PARTS + part).astype(jnp.int32)
    return pl.pallas_call(
        relayout_kernel,
        out_shape=jax.ShapeDtypeStruct((half, vecs, orbitals), BF16),
        grid_spec=pltpu.PrefetchScalarGridSpec(
            num_scalar_prefetch=1,
            grid=(half // depth, vecs // width),
            in_specs=[
                pl.BlockSpec(
                    (width, depth, orbitals), lambda i, g, c: (g, c[0] * (half // depth) + i, 0)
                )
            ],
            out_specs=pl.BlockSpec((depth, width, orbitals), lambda i, g, c: (i, g, 0)),
        ),
        cost_estimate=pl.CostEstimate(
            flops=0, bytes_accessed=4 * half * vecs * orbitals, transcendentals=0
        ),
        compiler_params=vmem_limit(),
        name="relayout",
    )(which.reshape(1), cholesky)


def bias_kernel(order, *refs, pieces, steps, last):
    greens, (kept, swapped), rest = refs[:pieces], refs[pieces : pieces + 2], refs[pieces + 2 :]
    before, rest = (rest[:2], rest[2:]) if last else ((), rest)
    outs, accs = (rest[:2], rest[2:]) if last else (rest, rest)
    step = pl.program_id(0)
    depth = kept.shape[0]
    fields = jnp.concatenate(
        [jnp.concatenate([g[i] for g in greens], axis=0) for i in range(depth)], axis=1
    )
    for side, (chol, acc) in enumerate(zip((kept, swapped), accs)):
        vectors = jnp.concatenate([chol[i] for i in range(depth)], axis=1)
        part = lax.dot_general(
            fields, vectors, (((1,), (1,)), ((), ())), preferred_element_type=F32
        )

        @pl.when(step == 0)
        def _():
            acc[...] = part + before[side][...] if last else part

        @pl.when(step > 0)
        def _():
            acc[...] += part

    if last:

        @pl.when(step == steps - 1)
        def _():
            for acc, out in zip(accs, outs):
                rows = out.shape[1] // (2 * pieces)
                for b in range(2 * pieces):
                    to = pl.ds(pl.multiple_of(order[b] * rows, rows), rows)
                    for c in range(CHUNKS):
                        first = (b * CHUNKS + c) * rows
                        out[c, to, :] = acc[first : first + rows, :].astype(out.dtype)


def bias_parts(order, greens, kept, swapped, part, before):
    rows_part, vecs, orbitals = kept.shape
    pieces = len(greens)
    walkers = pieces * greens[0].shape[1]
    last = part == PARTS - 1
    depth = min(8, rows_part)
    steps = rows_part // depth
    flat = pl.BlockSpec((walkers, vecs), lambda i, o: (0, 0))
    chol_spec = pl.BlockSpec((depth, vecs, orbitals), lambda i, o: (i, 0, 0))
    green_spec = pl.BlockSpec((depth,) + greens[0].shape[1:], lambda i, o: (i, 0, 0))
    by_chunk = (CHUNKS, walkers // CHUNKS, vecs)
    chunk_spec = pl.BlockSpec(by_chunk, lambda i, o: (0, 0, 0))
    wide = jax.ShapeDtypeStruct((walkers, vecs), F32)
    return pl.pallas_call(
        functools.partial(bias_kernel, pieces=pieces, steps=steps, last=last),
        out_shape=(
            (jax.ShapeDtypeStruct(by_chunk, F32), jax.ShapeDtypeStruct(by_chunk, BF16))
            if last
            else (wide, wide)
        ),
        grid_spec=pltpu.PrefetchScalarGridSpec(
            num_scalar_prefetch=1,
            grid=(steps,),
            in_specs=[green_spec] * pieces + [chol_spec] * 2 + [flat] * len(before),
            out_specs=(chunk_spec, chunk_spec) if last else (flat, flat),
            scratch_shapes=[pltpu.VMEM((walkers, vecs), F32)] * (2 if last else 0),
        ),
        cost_estimate=pl.CostEstimate(
            flops=4 * walkers * rows_part * vecs * orbitals,
            bytes_accessed=4 * rows_part * vecs * orbitals + 2 * walkers * rows_part * orbitals,
            transcendentals=0,
        ),
        compiler_params=vmem_limit(),
        name="bias",
    )(order, *greens, kept, swapped, *before)


def potential_kernel(order, *refs, pieces, steps):
    shift_kept, shift_swapped = refs[:2]
    kept, swapped = refs[2 : 2 + PARTS], refs[2 + PARTS : 2 + 2 * PARTS]
    outs, (field,) = refs[2 + 2 * PARTS : -1], refs[-1:]
    vecs = shift_kept.shape[1]
    blocks = 2 * pieces
    rows = field.shape[0] // blocks

    @pl.when(pl.program_id(0) == 0)
    def _():
        for b in range(blocks):
            at = pl.ds(pl.multiple_of(order[b] * rows, rows), rows)
            field[b * rows : (b + 1) * rows, :vecs] = shift_kept[at, :]
            field[b * rows : (b + 1) * rows, vecs:] = shift_swapped[at, :]

    for p in range(PARTS):

        @pl.when(pl.program_id(0) // steps == p)
        def _():
            for i in range(kept[p].shape[0]):
                vectors = jnp.concatenate([kept[p][i], swapped[p][i]], axis=0)
                part = jnp.dot(field[...], vectors, preferred_element_type=F32).astype(BF16)
                for j, out in enumerate(outs):
                    out[i] = part[2 * j * rows : 2 * (j + 1) * rows]


def potential_parts(order, shift_kept, shift_swapped, kept, swapped, pieces):
    rows_part, vecs, orbitals = kept[0].shape
    rows = PARTS * rows_part
    walkers = shift_kept.shape[0]
    depth = min(8, rows_part)
    steps = rows_part // depth
    chol_specs = [
        pl.BlockSpec(
            (depth, vecs, orbitals), lambda i, o, p=p: (jnp.clip(i - p * steps, 0, steps - 1), 0, 0)
        )
        for p in range(PARTS)
    ]
    shift_spec = pl.BlockSpec((walkers, vecs), lambda i, o: (0, 0))
    per = walkers // pieces
    return pl.pallas_call(
        functools.partial(potential_kernel, pieces=pieces, steps=steps),
        out_shape=[jax.ShapeDtypeStruct((rows, per, orbitals), BF16)] * pieces,
        grid_spec=pltpu.PrefetchScalarGridSpec(
            num_scalar_prefetch=1,
            grid=(rows // depth,),
            in_specs=[shift_spec] * 2 + chol_specs * 2,
            out_specs=[pl.BlockSpec((depth, per, orbitals), lambda i, o: (i, 0, 0))] * pieces,
            scratch_shapes=[pltpu.VMEM((walkers, 2 * vecs), BF16)],
        ),
        cost_estimate=pl.CostEstimate(
            flops=4 * walkers * rows * vecs * orbitals,
            bytes_accessed=4 * rows * vecs * orbitals + 2 * walkers * rows * orbitals,
            transcendentals=0,
        ),
        compiler_params=vmem_limit(),
        name="potential",
    )(order, shift_kept, shift_swapped, *kept, *swapped)


def taylor_kernel(order, *refs, groups):
    pots, terms = refs[:groups], refs[groups : 2 * groups]
    outs = refs[2 * groups : 3 * groups]
    full_pot, full_term, full_sum = refs[3 * groups :]
    low = pots[0].shape[2]
    high = terms[0].shape[1]
    for s, piece in enumerate(pots):
        for h in range(2):
            at = pl.ds(pl.multiple_of(order[2 * s + h] * low, low), low)
            full_pot[:, at, :] = piece[h]
    for s, piece in enumerate(terms):
        at = pl.ds(pl.multiple_of((order[2 * s] // 2) * high, high), high)
        full_term[:, at, :] = piece[...]
    count = full_pot.shape[0]
    now = [full_term[w] for w in range(count)]
    total = [None] * count
    for degree in range(1, TAYLOR + 1):
        for w in range(count):
            product = jnp.dot(full_pot[w], now[w], preferred_element_type=F32)
            now[w] = (product / degree).astype(BF16)
            wide = now[w].astype(F32)
            total[w] = wide if degree == 1 else total[w] + wide
    for w in range(count):
        full_sum[w] = total[w].astype(BF16)
    for s, out in enumerate(outs):
        at = pl.ds(pl.multiple_of((order[2 * s] // 2) * high, high), high)
        out[...] = full_sum[:, at, :]


def taylor_sums(order, pots, terms):
    groups = len(terms)
    _, count, _, orbitals = pots[0].shape
    high, occupied = terms[0].shape[1:]
    vmem = pl.BlockSpec(memory_space=pltpu.VMEM)
    return pl.pallas_call(
        functools.partial(taylor_kernel, groups=groups),
        out_shape=[jax.ShapeDtypeStruct((count, high, occupied), BF16)] * groups,
        in_specs=[pl.BlockSpec(memory_space=pltpu.SMEM)] + [vmem] * (2 * groups),
        out_specs=[vmem] * groups,
        scratch_shapes=[
            pltpu.VMEM((count, orbitals, orbitals), BF16),
            pltpu.VMEM((count, orbitals, occupied), BF16),
            pltpu.VMEM((count, orbitals, occupied), BF16),
        ],
        cost_estimate=pl.CostEstimate(
            flops=2 * TAYLOR * count * orbitals * orbitals * occupied,
            bytes_accessed=2 * count * orbitals * (orbitals + 2 * occupied),
            transcendentals=0,
        ),
        compiler_params=vmem_limit(),
        name="taylor",
    )(order, *pots, *terms)


def propagate(cholesky, green, aux_field, walker_orbitals):
    n_blk, n_rows = lax.axis_size("blk"), lax.axis_size("rows")
    me, plane = lax.axis_index("blk"), lax.axis_index("rows")
    core = me & 1
    vecs, rows_dev, orbitals = cholesky.shape
    walk_count, _, occupied = walker_orbitals.shape
    half = rows_dev // 2
    chips = n_blk // 2
    bits = chips.bit_length() - 1
    plane_bits = n_rows.bit_length() - 1
    mine = walk_count // CHUNKS
    each = mine // n_rows

    def swap_cores(x):
        return lax.ppermute(x, "blk", [(i, i ^ 1) for i in range(n_blk)])

    def swap_chips(x, t):
        pairs = [(i, i ^ (spread(i & 1, 1 << t, bits) << 1)) for i in range(n_blk)]
        return lax.ppermute(x, "blk", pairs)

    def swap_planes(x, s):
        return lax.ppermute(x, "rows", [(z, z ^ s) for z in range(n_rows)])

    tables = [
        [(spread(c, j, bits) << 1) | h for j in range(chips) for h in range(2)] for c in range(2)
    ]
    order = me ^ jnp.where(core == 0, jnp.array(tables[0], jnp.int32), jnp.array(tables[1], jnp.int32))
    plane_order = (plane * 2 + core) ^ jnp.arange(2 * n_rows, dtype=jnp.int32)

    def row_half(x, which):
        part = lax.dynamic_slice_in_dim(x, which * half, half, 1)
        return part.transpose(1, 0, 2)

    green_kept = row_half(green, core)
    green_swapped = swap_cores(row_half(green, 1 - core))
    rows_part = half // PARTS
    starts = []
    for p in range(PARTS):
        at = slice(p * rows_part, (p + 1) * rows_part)
        starts.append(jnp.concatenate([green_kept[at], green_swapped[at]], axis=1))
    cholesky, starts = lax.optimization_barrier((cholesky, starts))
    chol_swapped, chol_kept = [], []
    for p in range(PARTS):
        chol_sent = vectors_inner(cholesky, 1 - core, p)
        chol_swapped.append(swap_cores(chol_sent))
    for p in range(PARTS):
        chol_kept.append(vectors_inner(cholesky, core, p))

    own = walker_orbitals.reshape(CHUNKS, n_rows, each, rows_dev, occupied)
    terms = [
        lax.dynamic_index_in_dim(own, plane ^ s, 1, keepdims=False) for s in range(n_rows)
    ]
    terms = [swap_planes(x, s) if s else x for s, x in enumerate(terms)]

    def gather_green(p):
        gathered = [starts[p]]
        for t in range(bits):
            gathered += [swap_chips(piece, t) for piece in gathered]
        return gathered

    def full_bias(c, bias_kept, bias_swapped):
        bias = bias_kept[c] + bias_swapped[c].astype(F32)
        for t in range(plane_bits):
            bias = bias.astype(BF16)
            bias = bias.astype(F32) + swap_planes(bias, 1 << t).astype(F32)
        return bias

    def scatter_potential(c, bias):
        walkers = bias.shape[0]
        aux = aux_field.reshape(n_blk, walk_count, vecs)[:, c * mine : (c + 1) * mine]
        shifted = (time_root * (aux.reshape(walkers, vecs) - bias)).astype(BF16)
        shifted_swapped = swap_cores(shifted)
        acc = potential_parts(order, shifted, shifted_swapped, chol_kept, chol_swapped, chips)
        total = [a.astype(F32) for a in acc]
        for t in reversed(range(bits)):
            for j in reversed(range(1 << t)):
                sent = total[j + (1 << t)].astype(BF16)
                total[j] = total[j] + swap_chips(sent, t).astype(F32)
        potential = total[0].astype(BF16).transpose(1, 0, 2)
        return potential.reshape(2, n_rows, each, half, orbitals)

    def propagated(c, potential):
        swapped = swap_cores(potential[1])
        sides = jnp.stack([potential[0], swapped])
        pots = [
            lax.dynamic_index_in_dim(sides, plane ^ s, 1, keepdims=False) for s in range(n_rows)
        ]
        pots = [swap_planes(p, s) if s else p for s, p in enumerate(pots)]
        sums = taylor_sums(plane_order, pots, [t[c] for t in terms])
        result = jnp.zeros((n_rows, each, rows_dev, occupied), BF16)
        for s in range(n_rows):
            got = swap_planes(sums[s], s) if s else sums[s]
            result = lax.dynamic_update_index_in_dim(result, got, plane ^ s, 0)
        return result.reshape(mine, rows_dev, occupied)

    gathered = [gather_green(p) for p in range(PARTS)]
    parts = ()
    for p in range(PARTS):
        parts = bias_parts(order, gathered[p], chol_kept[p], chol_swapped[p], p, parts)
    bias_kept, bias_swapped = parts[0], swap_cores(parts[1])
    biases = [full_bias(c, bias_kept, bias_swapped) for c in range(CHUNKS)]
    potentials = [scatter_potential(c, biases[c]) for c in range(CHUNKS)]
    sums = jnp.concatenate([propagated(c, potentials[c]) for c in range(CHUNKS)], axis=0)
    force_bias = jnp.stack([b.reshape(n_blk, mine, vecs) for b in biases], axis=1)
    force_bias = force_bias.reshape(-1, vecs)
    return walker_orbitals.astype(F32) + sums.astype(F32), force_bias


def solution(mesh):
    return jax.shard_map(
        propagate,
        mesh=mesh,
        in_specs=(
            P("blk", "rows", None),
            P("blk", "rows", None),
            P(None, "blk"),
            P("blk", "rows", None),
        ),
        out_specs=(P("blk", "rows", None), P(None, "blk")),
        check_vma=False,
    )
```

```python
import functools

import jax
import jax.numpy as jnp
from jax import lax
from jax.experimental import pallas as pl
from jax.experimental.pallas import tpu as pltpu
from jax.sharding import PartitionSpec as P


TAYLOR = 4
CHUNKS = 2
PARTS = 2
BIAS_DEPTH = 8
DEPTH = 8

time_root = 0.5
F32, BF16 = jnp.float32, jnp.bfloat16


def spread(core, rel, bits):
    if core == 0:
        return rel
    return sum(((rel >> t) & 1) << (bits - 1 - t) for t in range(bits))


def in_hbm(arrays):
    return [pltpu.with_memory_space_constraint(x, pltpu.HBM) for x in arrays]


def vmem_limit():
    return pltpu.CompilerParams(vmem_limit_bytes=56 << 20)


def relayout_kernel(which, block, out):
    out[...] = jnp.swapaxes(block[...], 0, 1)


def vectors_inner(cholesky, which, part):
    vecs, rows, orbitals = cholesky.shape
    half = rows // 2 // PARTS
    depth, width = min(16, half), min(256, vecs)
    which = (which * PARTS + part).astype(jnp.int32)
    return pl.pallas_call(
        relayout_kernel,
        out_shape=jax.ShapeDtypeStruct((half, vecs, orbitals), BF16),
        grid_spec=pltpu.PrefetchScalarGridSpec(
            num_scalar_prefetch=1,
            grid=(half // depth, vecs // width),
            in_specs=[
                pl.BlockSpec(
                    (width, depth, orbitals), lambda i, g, c: (g, c[0] * (half // depth) + i, 0)
                )
            ],
            out_specs=pl.BlockSpec((depth, width, orbitals), lambda i, g, c: (i, g, 0)),
        ),
        cost_estimate=pl.CostEstimate(
            flops=0, bytes_accessed=4 * half * vecs * orbitals, transcendentals=0
        ),
        compiler_params=vmem_limit(),
        name="relayout",
    )(which.reshape(1), cholesky)


def bias_kernel(order, *refs, pieces, steps, last):
    greens, (kept, swapped), rest = refs[:pieces], refs[pieces : pieces + 2], refs[pieces + 2 :]
    before, rest = (rest[:2], rest[2:]) if last else ((), rest)
    outs, accs = (rest[:2], rest[2:]) if last else (rest, rest)
    step = pl.program_id(0)
    depth = kept.shape[0]
    fields = jnp.concatenate(
        [jnp.concatenate([g[i] for g in greens], axis=0) for i in range(depth)], axis=1
    )
    for side, (chol, acc) in enumerate(zip((kept, swapped), accs)):
        vectors = jnp.concatenate([chol[i] for i in range(depth)], axis=1)
        part = lax.dot_general(
            fields, vectors, (((1,), (1,)), ((), ())), preferred_element_type=F32
        )

        @pl.when(step == 0)
        def _():
            acc[...] = part + before[side][...] if last else part

        @pl.when(step > 0)
        def _():
            acc[...] += part

    if last:

        @pl.when(step == steps - 1)
        def _():
            for acc, out in zip(accs, outs):
                rows = out.shape[1] // (2 * pieces)
                for b in range(2 * pieces):
                    to = pl.ds(pl.multiple_of(order[b] * rows, rows), rows)
                    for c in range(CHUNKS):
                        first = (b * CHUNKS + c) * rows
                        out[c, to, :] = acc[first : first + rows, :].astype(out.dtype)


def bias_parts(order, greens, kept, swapped, part, before):
    rows_part, vecs, orbitals = kept.shape
    pieces = len(greens)
    walkers = pieces * greens[0].shape[1]
    last = part == PARTS - 1
    depth = min(BIAS_DEPTH, rows_part)
    steps = rows_part // depth
    flat = pl.BlockSpec((walkers, vecs), lambda i, o: (0, 0))
    chol_spec = pl.BlockSpec((depth, vecs, orbitals), lambda i, o: (i, 0, 0))
    green_spec = pl.BlockSpec((depth,) + greens[0].shape[1:], lambda i, o: (i, 0, 0))
    by_chunk = (CHUNKS, walkers // CHUNKS, vecs)
    chunk_spec = pl.BlockSpec(by_chunk, lambda i, o: (0, 0, 0))
    wide = jax.ShapeDtypeStruct((walkers, vecs), F32)
    return pl.pallas_call(
        functools.partial(bias_kernel, pieces=pieces, steps=steps, last=last),
        out_shape=(
            (jax.ShapeDtypeStruct(by_chunk, F32), jax.ShapeDtypeStruct(by_chunk, BF16))
            if last
            else (wide, wide)
        ),
        grid_spec=pltpu.PrefetchScalarGridSpec(
            num_scalar_prefetch=1,
            grid=(steps,),
            in_specs=[green_spec] * pieces + [chol_spec] * 2 + [flat] * len(before),
            out_specs=(chunk_spec, chunk_spec) if last else (flat, flat),
            scratch_shapes=[pltpu.VMEM((walkers, vecs), F32)] * (2 if last else 0),
        ),
        cost_estimate=pl.CostEstimate(
            flops=4 * walkers * rows_part * vecs * orbitals,
            bytes_accessed=4 * rows_part * vecs * orbitals + 2 * walkers * rows_part * orbitals,
            transcendentals=0,
        ),
        compiler_params=vmem_limit(),
        name="bias",
    )(order, *in_hbm(greens), kept, swapped, *in_hbm(before))


def potential_kernel(order, shift_kept, shift_swapped, *refs, pieces, depth, firsts):
    kept, swapped = refs[:PARTS], refs[PARTS : 2 * PARTS]
    outs, (field, vectors, made, arrived, left) = refs[2 * PARTS : -5], refs[-5:]
    vecs = shift_kept.shape[1]
    blocks = 2 * pieces
    rows = field.shape[0] // blocks
    per = made.shape[1] // pieces
    steps = firsts[-1]

    def fetch(step, act):
        slot = lax.rem(step, 2)
        for p in range(PARTS):

            @pl.when((step >= firsts[p]) & (step < firsts[p + 1]))
            def _():
                at = pl.ds((step - firsts[p]) * depth, depth)
                for side, source in enumerate((kept[p], swapped[p])):
                    to = vectors.at[slot, :, side * vecs : (side + 1) * vecs]
                    act(pltpu.make_async_copy(source.at[at], to, arrived.at[slot, side]))

    fetch(0, lambda copy: copy.start())
    for b in range(blocks):
        at = pl.ds(pl.multiple_of(order[b] * rows, rows), rows)
        field[b * rows : (b + 1) * rows, :vecs] = shift_kept[at, :]
        field[b * rows : (b + 1) * rows, vecs:] = shift_swapped[at, :]

    def put(step, act):
        at = pl.ds(step * depth, depth)
        for j, out in enumerate(outs):
            source = made.at[at, j * per : (j + 1) * per]
            act(pltpu.make_async_copy(source, out.at[at], left.at[step, j]))

    def one(step, carry):
        fetch(step + 1, lambda copy: copy.start())
        fetch(step, lambda copy: copy.wait())
        slot = lax.rem(step, 2)
        for i in range(depth):
            part = jnp.dot(field[...], vectors[slot, i], preferred_element_type=F32)
            made[step * depth + i] = part.astype(BF16)
        put(step, lambda copy: copy.start())
        return carry

    lax.fori_loop(0, steps, one, 0)
    for step in range(steps):
        put(step, lambda copy: copy.wait())


def potential_parts(order, shift_kept, shift_swapped, kept, swapped, pieces):
    vecs, orbitals = kept[0].shape[1:]
    walkers = shift_kept.shape[0]
    depth = min(DEPTH, min(x.shape[0] for x in kept))
    firsts = [sum(x.shape[0] for x in kept[:p]) // depth for p in range(PARTS + 1)]
    rows = firsts[-1] * depth
    vmem, hbm = pl.BlockSpec(memory_space=pltpu.VMEM), pl.BlockSpec(memory_space=pl.ANY)
    per = walkers // pieces
    return pl.pallas_call(
        functools.partial(potential_kernel, pieces=pieces, depth=depth, firsts=firsts),
        out_shape=[jax.ShapeDtypeStruct((rows, per, orbitals), BF16)] * pieces,
        in_specs=[pl.BlockSpec(memory_space=pltpu.SMEM)] + [vmem] * 2 + [hbm] * (2 * PARTS),
        out_specs=[hbm] * pieces,
        scratch_shapes=[
            pltpu.VMEM((walkers, 2 * vecs), BF16),
            pltpu.VMEM((2, depth, 2 * vecs, orbitals), BF16),
            pltpu.VMEM((rows, walkers, orbitals), BF16),
            pltpu.SemaphoreType.DMA((2, 2)),
            pltpu.SemaphoreType.DMA((rows // depth, pieces)),
        ],
        cost_estimate=pl.CostEstimate(
            flops=4 * walkers * rows * vecs * orbitals,
            bytes_accessed=4 * rows * vecs * orbitals + 2 * walkers * rows * orbitals,
            transcendentals=0,
        ),
        compiler_params=vmem_limit(),
        name="potential",
    )(order, shift_kept, shift_swapped, *kept, *swapped)


def taylor_kernel(order, *refs, groups):
    pots, terms = refs[:groups], refs[groups : 2 * groups]
    outs = refs[2 * groups : 3 * groups]
    full_pot, full_term, full_sum = refs[3 * groups :]
    low = pots[0].shape[2]
    high = terms[0].shape[2]
    for s, piece in enumerate(pots):
        for h in range(2):
            at = pl.ds(pl.multiple_of(order[2 * s + h] * low, low), low)
            full_pot[:, at, :] = piece[h]
    for s, piece in enumerate(terms):
        at = pl.ds(pl.multiple_of((order[2 * s] // 2) * high, high), high)
        full_term[:, at, :] = piece[0]
    count = full_pot.shape[0]
    now = [full_term[w] for w in range(count)]
    total = [None] * count
    for degree in range(1, TAYLOR + 1):
        for w in range(count):
            product = jnp.dot(full_pot[w], now[w], preferred_element_type=F32)
            now[w] = (product / degree).astype(BF16)
            wide = now[w].astype(F32)
            total[w] = wide if degree == 1 else total[w] + wide
    for w in range(count):
        full_sum[w] = total[w].astype(BF16)
    for s, out in enumerate(outs):
        at = pl.ds(pl.multiple_of((order[2 * s] // 2) * high, high), high)
        out[...] = full_sum[:, at, :]


def taylor_sums(order, chunk, pots, terms):
    groups = len(terms)
    _, count, low, orbitals = pots[0].shape
    _, _, high, occupied = terms[0].shape
    pot_spec = pl.BlockSpec((2, count, low, orbitals), lambda i: (0, 0, 0, 0))
    term_spec = pl.BlockSpec((1, count, high, occupied), lambda i: (chunk, 0, 0, 0))
    out_spec = pl.BlockSpec((count, high, occupied), lambda i: (0, 0, 0))
    return pl.pallas_call(
        functools.partial(taylor_kernel, groups=groups),
        out_shape=[jax.ShapeDtypeStruct((count, high, occupied), BF16)] * groups,
        grid=(1,),
        in_specs=[pl.BlockSpec(memory_space=pltpu.SMEM)]
        + [pot_spec] * groups
        + [term_spec] * groups,
        out_specs=[out_spec] * groups,
        scratch_shapes=[
            pltpu.VMEM((count, orbitals, orbitals), BF16),
            pltpu.VMEM((count, orbitals, occupied), BF16),
            pltpu.VMEM((count, orbitals, occupied), BF16),
        ],
        cost_estimate=pl.CostEstimate(
            flops=2 * TAYLOR * count * orbitals * orbitals * occupied,
            bytes_accessed=2 * count * orbitals * (orbitals + 2 * occupied),
            transcendentals=0,
        ),
        compiler_params=vmem_limit(),
        name="taylor",
    )(order, *in_hbm(pots), *in_hbm(terms))


def propagate(cholesky, green, aux_field, walker_orbitals):
    n_blk, n_rows = lax.axis_size("blk"), lax.axis_size("rows")
    me, plane = lax.axis_index("blk"), lax.axis_index("rows")
    core = me & 1
    vecs, rows_dev, orbitals = cholesky.shape
    walk_count, _, occupied = walker_orbitals.shape
    half = rows_dev // 2
    chips = n_blk // 2
    bits = chips.bit_length() - 1
    plane_bits = n_rows.bit_length() - 1
    mine = walk_count // CHUNKS
    each = mine // n_rows

    def swap_cores(x):
        return lax.ppermute(x, "blk", [(i, i ^ 1) for i in range(n_blk)])

    def swap_chips(x, t):
        pairs = [(i, i ^ (spread(i & 1, 1 << t, bits) << 1)) for i in range(n_blk)]
        return lax.ppermute(x, "blk", pairs)

    def swap_planes(x, s):
        return lax.ppermute(x, "rows", [(z, z ^ s) for z in range(n_rows)])

    tables = [
        [(spread(c, j, bits) << 1) | h for j in range(chips) for h in range(2)] for c in range(2)
    ]
    order = me ^ jnp.where(core == 0, jnp.array(tables[0], jnp.int32), jnp.array(tables[1], jnp.int32))
    plane_order = (plane * 2 + core) ^ jnp.arange(2 * n_rows, dtype=jnp.int32)

    def row_half(x, which):
        part = lax.dynamic_slice_in_dim(x, which * half, half, 1)
        return part.transpose(1, 0, 2)

    green_kept = row_half(green, core)
    green_swapped = swap_cores(row_half(green, 1 - core))
    rows_part = half // PARTS
    starts = []
    for p in range(PARTS):
        at = slice(p * rows_part, (p + 1) * rows_part)
        starts.append(jnp.concatenate([green_kept[at], green_swapped[at]], axis=1))
    cholesky, starts = lax.optimization_barrier((cholesky, starts))
    chol_swapped, chol_kept = [], []
    for p in range(PARTS):
        chol_sent = vectors_inner(cholesky, 1 - core, p)
        chol_swapped.append(swap_cores(chol_sent))
    for p in range(PARTS):
        chol_kept.append(vectors_inner(cholesky, core, p))

    own = walker_orbitals.reshape(CHUNKS, n_rows, each, rows_dev, occupied)
    terms = [
        lax.dynamic_index_in_dim(own, plane ^ s, 1, keepdims=False) for s in range(n_rows)
    ]
    terms = [swap_planes(x, s) if s else x for s, x in enumerate(terms)]

    def gather_green(p):
        gathered = [starts[p]]
        for t in range(bits):
            gathered += [swap_chips(piece, t) for piece in gathered]
        return gathered

    def full_bias(c, bias_kept, bias_swapped):
        bias = bias_kept[c] + bias_swapped[c].astype(F32)
        for t in range(plane_bits):
            bias = bias.astype(BF16)
            bias = bias.astype(F32) + swap_planes(bias, 1 << t).astype(F32)
        return bias

    def scatter_potential(c, bias):
        walkers = bias.shape[0]
        aux = aux_field.reshape(n_blk, walk_count, vecs)[:, c * mine : (c + 1) * mine]
        shifted = (time_root * (aux.reshape(walkers, vecs) - bias)).astype(BF16)
        shifted_swapped = swap_cores(shifted)
        acc = potential_parts(order, shifted, shifted_swapped, chol_kept, chol_swapped, chips)
        total = [a.astype(F32) for a in acc]
        for t in reversed(range(bits)):
            for j in reversed(range(1 << t)):
                sent = total[j + (1 << t)].astype(BF16)
                total[j] = total[j] + swap_chips(sent, t).astype(F32)
        potential = total[0].astype(BF16).transpose(1, 0, 2)
        return potential.reshape(2, n_rows, each, half, orbitals)

    def propagated(c, potential):
        swapped = swap_cores(potential[1])
        sides = jnp.stack([potential[0], swapped])
        pots = [
            lax.dynamic_index_in_dim(sides, plane ^ s, 1, keepdims=False) for s in range(n_rows)
        ]
        pots = [swap_planes(p, s) if s else p for s, p in enumerate(pots)]
        sums = taylor_sums(plane_order, c, pots, terms)
        result = jnp.zeros((n_rows, each, rows_dev, occupied), BF16)
        for s in range(n_rows):
            got = swap_planes(sums[s], s) if s else sums[s]
            result = lax.dynamic_update_index_in_dim(result, got, plane ^ s, 0)
        return result.reshape(mine, rows_dev, occupied)

    gathered = [gather_green(p) for p in range(PARTS)]
    parts = ()
    for p in range(PARTS):
        parts = bias_parts(order, gathered[p], chol_kept[p], chol_swapped[p], p, parts)
    bias_kept, bias_swapped = parts[0], swap_cores(parts[1])
    biases = [full_bias(c, bias_kept, bias_swapped) for c in range(CHUNKS)]
    potentials = [scatter_potential(c, biases[c]) for c in range(CHUNKS)]
    sums = jnp.concatenate([propagated(c, potentials[c]) for c in range(CHUNKS)], axis=0)
    force_bias = jnp.stack([b.reshape(n_blk, mine, vecs) for b in biases], axis=1)
    force_bias = force_bias.reshape(-1, vecs)
    return walker_orbitals.astype(F32) + sums.astype(F32), force_bias


def solution(mesh):
    return jax.shard_map(
        propagate,
        mesh=mesh,
        in_specs=(
            P("blk", "rows", None),
            P("blk", "rows", None),
            P(None, "blk"),
            P("blk", "rows", None),
        ),
        out_specs=(P("blk", "rows", None), P(None, "blk")),
        check_vma=False,
    )
```
